128 devices in a mesh: ctx: 32 (over z_lo, y, x), head: 4 (over z_hi, core).
Axes of the slice: x: 4, y: 4, z: 4 (z_hi: 2, z_lo: 2; z = z_hi * 2 + z_lo), core: 2. Of those that a mesh axis runs over, the one named last changes fastest.
Arguments:
- queries: bfloat16 [1024, 16384], P('ctx', 'head'), may hold values from -512 to 512
- kv_cache: bfloat16 [2, 16384, 1024], P(None, 'ctx', 'head'), may hold values from -7 to 7
- fill_len: int32 [32], P('ctx'), may hold values from 64 to 512
- prompt_offset: int32 [1], replicated, may hold values from 8192 to 15360
Outputs:
- attended: bfloat16 [1024, 16384], P(('ctx', 'head'))
The draws below stay inside these ranges and needn't reach their ends.
All inputs are finite; a program needn't handle non-finite values.
Results may differ from the reference program's by a relative error of at most 0.0045.
Values may be sent and summed in bfloat16 or wider, within the bound.
No kernel may reach another device: no remote copies, remote signals or barrier semaphores. Data moves between devices by JAX's collectives and lax.ppermute only.
A program may use at most 192 MiB of HBM per device.

```python
import math
import jax
import jax.numpy as jnp
from jax import lax

HEADS = 128
KV_HEADS = 8
HEAD_DIM = 128
SLOTS = 512
CACHE = 16384
PROMPT = 1024
N_CTX = 32


def base_keys(key):
    normal_keys = jnp.clip(jax.random.normal(jax.random.fold_in(key, 11), (CACHE, KV_HEADS * HEAD_DIM), jnp.float32), -5.0, 5.0)
    row_scale = jnp.exp(jax.random.uniform(jax.random.fold_in(key, 13), (CACHE, 1), jnp.float32, math.log(0.7), math.log(1.4)))
    return normal_keys * row_scale


def draw_kv_cache(key, part):
    key_rows = base_keys(key)
    value_rows = jnp.clip(jax.random.normal(jax.random.fold_in(key, 12), (CACHE, KV_HEADS * HEAD_DIM), jnp.float32), -6.0, 6.0)
    return jnp.stack([key_rows, value_rows]).astype(jnp.bfloat16)


def draw_queries(key, part):
    shape_all = (PROMPT, HEADS * HEAD_DIM)
    drawn = jnp.clip(jax.random.normal(jax.random.fold_in(key, 21), shape_all, jnp.float32), -6.0, 6.0)
    drawn = drawn * jnp.exp(jax.random.uniform(jax.random.fold_in(key, 23), (PROMPT, 1), jnp.float32, 0.0, math.log(6.0)))
    return jnp.clip(drawn, -512.0, 512.0).astype(jnp.bfloat16)


def touch_ends(entries, own_key, low, high):
    place = [jax.random.randint(jax.random.fold_in(own_key, axis), (), 0, length) for axis, length in enumerate(entries.shape)]
    widest = entries.shape.index(max(entries.shape))
    beside = place[:widest] + [(place[widest] + 1) % entries.shape[widest]] + place[widest + 1:]
    return entries.at[tuple(place)].set(low).at[tuple(beside)].set(high)


def setup_inputs(seed: int = 0) -> dict:
    arg_keys = jax.random.split(jax.random.key(seed), 5)
    queries = draw_queries(jax.random.fold_in(arg_keys[4], 71), 0)
    kv_cache = draw_kv_cache(jax.random.fold_in(arg_keys[4], 71), 0)
    fill_len = touch_ends(jax.random.randint(arg_keys[2], (N_CTX,), SLOTS // 8, SLOTS + 1), jax.random.fold_in(arg_keys[2], 1), SLOTS // 8, SLOTS).astype(jnp.int32)
    prompt_offset = jax.random.randint(arg_keys[3], (1,), (N_CTX // 2) * SLOTS, CACHE - PROMPT + 1).astype(jnp.int32)
    return dict(queries=queries, kv_cache=kv_cache, fill_len=fill_len, prompt_offset=prompt_offset)


def ref_partial(query_groups, key_block, value_block, allowed):
    scaling = 1.0 / math.sqrt(HEAD_DIM)
    scores = jnp.einsum('nhgd,khd->hgnk', query_groups, key_block) * scaling
    scores = jnp.where(allowed[None, None], scores, -1e+30)
    row_max = lax.optimization_barrier(jnp.max(scores, axis=-1))
    weights = jnp.exp(scores - row_max[..., None])
    row_sum = lax.optimization_barrier(jnp.sum(weights, axis=-1))
    rounded = lax.optimization_barrier(weights.astype(jnp.bfloat16)).astype(jnp.float32)
    weighted = jnp.einsum('hgnk,khd->nhgd', rounded, value_block)
    weighted = weighted / jnp.transpose(row_sum, (2, 0, 1))[..., None]
    row_count = query_groups.shape[0]
    partial_value = lax.optimization_barrier(weighted.astype(jnp.bfloat16)).astype(jnp.float32)
    partial_value = partial_value.reshape(row_count, HEADS, HEAD_DIM)
    log_total = jnp.transpose(row_max + jnp.log(row_sum), (2, 0, 1)).reshape(row_count, HEADS)
    return (partial_value, log_total)

def reference(queries, kv_cache, fill_len, prompt_offset):
    groups = HEADS // KV_HEADS
    query_groups = queries.astype(jnp.float32).reshape(PROMPT, KV_HEADS, groups, HEAD_DIM)
    query_pos = prompt_offset[0] + jnp.arange(PROMPT, dtype=jnp.int32)
    key_shards = kv_cache[0].reshape(N_CTX, SLOTS, KV_HEADS, HEAD_DIM)
    value_shards = kv_cache[1].reshape(N_CTX, SLOTS, KV_HEADS, HEAD_DIM)
    slot_ids = jnp.arange(SLOTS, dtype=jnp.int32)

    def one_shard(running, inputs):
        key_block, value_block, shard_fill, shard_idx = inputs
        slot_pos = shard_idx * SLOTS + slot_ids
        allowed = (slot_ids < shard_fill)[None, :] & (slot_pos[None, :] <= query_pos[:, None])
        partial_value, log_total = ref_partial(query_groups, key_block.astype(jnp.float32), value_block.astype(jnp.float32), allowed)
        running_max, running_sum, running_acc = running
        new_max = jnp.maximum(running_max, log_total)
        old_scale = jnp.exp(running_max - new_max)
        new_scale = jnp.exp(log_total - new_max)
        return ((new_max, running_sum * old_scale + new_scale, running_acc * old_scale[..., None] + new_scale[..., None] * partial_value), None)
    initial = (jnp.full((PROMPT, HEADS), -1e+30, jnp.float32), jnp.zeros((PROMPT, HEADS), jnp.float32), jnp.zeros((PROMPT, HEADS, HEAD_DIM), jnp.float32))
    final_state, ignored = lax.scan(one_shard, initial, (key_shards, value_shards, fill_len, jnp.arange(N_CTX, dtype=jnp.int32)))
    final_max, final_sum, final_acc = final_state
    return (final_acc / final_sum[..., None]).reshape(PROMPT, HEADS * HEAD_DIM).astype(jnp.bfloat16)
```

```python
import math

import jax
import jax.numpy as jnp
from jax import lax
from jax.experimental import pallas as pl
from jax.experimental.pallas import tpu as pltpu
from jax.sharding import Mesh, PartitionSpec as P

HEAD_DIM = 128
SLOTS = 512
BLOCK = 256
SCALING = 1.0 / math.sqrt(HEAD_DIM)
LOG2E = math.log2(math.e)
MASKED = -1e30


def attend_kernel(info, *refs):
    q_refs, kv_refs, out_ref = refs[:8], refs[8:12], refs[12]
    kbuf, vbuf, logs, thr = refs[13:]
    zl, y, x, offset = info[0], info[1], info[2], info[3]
    last_token = offset + (16 + 4 * y + 3) * 32 + 31
    shard, fill, room = [], [], []
    for k in range(4):
        j = zl * 16 + ((y + 4 - k) & 3) * 4 + x
        code = kv_refs[k][1024:1040, 0:128].astype(jnp.float32)
        n = jnp.max(code[0:8]).astype(jnp.int32) * 16 + jnp.max(code[8:16]).astype(jnp.int32)
        n = jnp.where(j * SLOTS > last_token, 0, n)
        shard.append(j)
        fill.append(n)
        room.append(((n + 15) // 16) * 16)
    start = []
    for k in range(4):
        before = 0
        for o in range(4):
            if o != k:
                before = before + jnp.where(shard[o] < shard[k], room[o], 0)
        start.append(before)
    total = room[0] + room[1] + room[2] + room[3]
    edge_shard, edge_start = jnp.int32(-1), jnp.int32(0)
    for k in range(4):
        later = (fill[k] > 0) & (shard[k] > edge_shard)
        edge_start = jnp.where(later, start[k], edge_start)
        edge_shard = jnp.where(later, shard[k], edge_shard)
    causal = edge_shard * SLOTS + (SLOTS - 1) > offset

    row = lax.broadcasted_iota(jnp.int32, (SLOTS, HEAD_DIM), 0)
    ones = jnp.ones((SLOTS, HEAD_DIM), jnp.bfloat16)
    zeros = jnp.zeros((SLOTS, HEAD_DIM), jnp.bfloat16)
    for step in range(4):
        yy = step
        for k in range(4):

            @pl.when(((y + 4 - k) & 3) == yy)
            def _(k=k):
                live = row < fill[k]
                at = pl.ds(pl.multiple_of(start[k], 16), SLOTS)
                for h in range(2):
                    cols = slice(h * HEAD_DIM, (h + 1) * HEAD_DIM)
                    keys = kv_refs[k][0:SLOTS, cols]
                    first = jnp.broadcast_to(kv_refs[k][0:1, cols], keys.shape)
                    kbuf[h, at, :] = jnp.where(live, keys, first)
                    vbuf[h, at, 0:HEAD_DIM] = jnp.where(live, kv_refs[k][SLOTS : 2 * SLOTS, cols], zeros)
                    vbuf[h, at, HEAD_DIM : 2 * HEAD_DIM] = jnp.where(live, ones, zeros)
                    tail = pl.ds(pl.multiple_of(start[k] + SLOTS, 16), BLOCK)
                    kbuf[h, tail, :] = first[0:BLOCK]
                    vbuf[h, tail, 0:HEAD_DIM] = zeros[0:BLOCK]
                    vbuf[h, tail, HEAD_DIM : 2 * HEAD_DIM] = zeros[0:BLOCK]

    place = []
    token = lax.broadcasted_iota(jnp.int32, (32, HEAD_DIM), 0)
    for i in range(8):
        tz = zl if i < 4 else 1 - zl
        tx = (x + 4 - (i & 3)) & 3
        place.append(pl.multiple_of((tz * 4 + tx) * 32, 32))
        position = offset + (tz * 16 + y * 4 + tx) * 32 + token
        thr[32 * i : 32 * i + 32, :] = jnp.maximum(position - edge_shard * SLOTS, -1) + edge_start
    logs[...] = jnp.zeros_like(logs)
    lane = lax.broadcasted_iota(jnp.int32, (256, HEAD_DIM), 1)

    def run(blocks, masked):
        width = blocks * BLOCK

        def head(h, carry):
            group = h // 16
            cols = pl.ds(pl.multiple_of(h * HEAD_DIM, HEAD_DIM), HEAD_DIM)
            query = jnp.concatenate([ref[:, cols] for ref in q_refs], axis=0)
            scores = lax.dot_general(
                query, kbuf[group, 0:width, :], (((1,), (1,)), ((), ())), preferred_element_type=jnp.float32
            )
            tiles = [scores[:, 128 * t : 128 * t + 128] for t in range(width // 128)]
            if masked:
                limit = thr[...]
                for t in range(max(0, width // 128 - 6), width // 128):
                    tiles[t] = jnp.where(lane > limit - 128 * t, MASKED, tiles[t])
            peak = tiles[0]
            for tile in tiles[1:]:
                peak = jnp.maximum(peak, tile)
            peak = jnp.max(peak, axis=1, keepdims=True)
            if masked:
                peak = jnp.maximum(peak, 0.1 * MASKED)
            peak = jnp.broadcast_to(peak, (256, HEAD_DIM))
            weights = [jnp.exp2((tile - peak) * (SCALING * LOG2E)).astype(jnp.bfloat16) for tile in tiles]
            weights = jnp.concatenate(weights, axis=1)
            both = jnp.dot(weights, vbuf[group, 0:width, :], preferred_element_type=jnp.float32)
            mass = both[:, HEAD_DIM : 2 * HEAD_DIM]
            seen = mass > 0.0
            mass = jnp.where(seen, mass, 1.0)
            partial = (both[:, 0:HEAD_DIM] / mass).astype(jnp.bfloat16)
            for i in range(8):
                out_ref[pl.ds(place[i], 32), cols] = partial[32 * i : 32 * i + 32]
            log_total = jnp.where(seen, peak * SCALING + jnp.log(mass), MASKED)
            logs[...] = jnp.where(lane == h, log_total, logs[...])
            return carry

        lax.fori_loop(0, 32, head, 0)

    count = jnp.maximum((total + BLOCK - 1) // BLOCK, 1)
    for blocks in range(1, 9):
        for masked in (False, True):

            @pl.when((count == blocks) & (causal == masked))
            def _(blocks=blocks, masked=masked):
                run(blocks, masked)

    value = logs[...]
    high = value.astype(jnp.bfloat16).astype(jnp.float32)
    rest = value - high
    middle = rest.astype(jnp.bfloat16).astype(jnp.float32)
    low = (rest - middle).astype(jnp.bfloat16).astype(jnp.float32)
    packed = (high + pltpu.roll(middle, 32, 1) + pltpu.roll(low, 64, 1)).astype(jnp.bfloat16)
    for i in range(8):
        out_ref[pl.ds(place[i], 32), 4096:4224] = packed[32 * i : 32 * i + 32]


def attend(info, q_pieces, kv_pieces):
    return pl.pallas_call(
        attend_kernel,
        out_shape=jax.ShapeDtypeStruct((256, 4224), jnp.bfloat16),
        in_specs=[pl.BlockSpec(memory_space=pltpu.SMEM)] + [pl.BlockSpec(memory_space=pltpu.VMEM)] * 12,
        out_specs=pl.BlockSpec(memory_space=pltpu.VMEM),
        scratch_shapes=[
            pltpu.VMEM((2, 4 * SLOTS + BLOCK, HEAD_DIM), jnp.bfloat16),
            pltpu.VMEM((2, 4 * SLOTS + BLOCK, 2 * HEAD_DIM), jnp.bfloat16),
            pltpu.VMEM((256, HEAD_DIM), jnp.float32),
            pltpu.VMEM((256, HEAD_DIM), jnp.int32),
        ],
        name="attend",
    )(info, *q_pieces, *kv_pieces)


def merge_kernel(in_ref, out_ref):
    totals = []
    for s in range(8):
        code = in_ref[s, 0, :, 4096:4224].astype(jnp.float32)
        totals.append(code + pltpu.roll(code, 96, 1) + pltpu.roll(code, 64, 1))
    peak = totals[0]
    for t in totals[1:]:
        peak = jnp.maximum(peak, t)
    shares = [jnp.exp(t - peak) for t in totals]
    mass = shares[0]
    for s in shares[1:]:
        mass = mass + s
    shares = [s / mass for s in shares]
    for h in range(32):
        cols = slice(h * HEAD_DIM, (h + 1) * HEAD_DIM)
        acc = jnp.zeros((8, HEAD_DIM), jnp.float32)
        for s in range(8):
            share = jnp.broadcast_to(shares[s][:, h : h + 1], (8, HEAD_DIM))
            acc = acc + share * in_ref[s, 0, :, cols].astype(jnp.float32)
        out_ref[:, cols] = acc.astype(jnp.bfloat16)


def merge(received):
    return pl.pallas_call(
        merge_kernel,
        grid=(4,),
        out_shape=jax.ShapeDtypeStruct((8, 16384), jnp.bfloat16),
        in_specs=[pl.BlockSpec((8, 1, 8, 4224), lambda g: (0, g, 0, 0))],
        out_specs=pl.BlockSpec((8, 4096), lambda g: (0, g)),
        name="merge",
    )(received)


def shift(value, axis, by):
    size = lax.axis_size(axis)
    return lax.ppermute(value, axis, [(i, (i + by) % size) for i in range(size)])


def per_device(queries, kv_cache, fill_len, prompt_offset):
    fill = fill_len[0]
    code = jnp.concatenate(
        [jnp.full((8, 256), fill // 16, jnp.bfloat16), jnp.full((8, 256), fill % 16, jnp.bfloat16)], axis=0
    )
    cache = jnp.concatenate([kv_cache.reshape(1024, 256), code], axis=0)
    info = jnp.stack([lax.axis_index("zl"), lax.axis_index("y"), lax.axis_index("x"), prompt_offset[0]])
    across = shift(queries, "zl", 1)
    kv_pieces = [cache] + [shift(cache, "y", k) for k in (1, 2, 3)]
    q_pieces = [queries] + [shift(queries, "x", k) for k in (1, 2, 3)]
    q_pieces += [across] + [shift(across, "x", k) for k in (1, 2, 3)]
    partial = attend(info.astype(jnp.int32), q_pieces, kv_pieces)
    received = lax.all_to_all(
        partial.reshape(32, 8, 4224), ("zl", "x", "zh", "core"), split_axis=0, concat_axis=0, tiled=True
    )
    return merge(received.reshape(8, 4, 8, 4224))


def solution(mesh):
    split = Mesh(mesh.devices.reshape(2, 4, 4, 2, 2), ("zl", "y", "x", "zh", "core"))
    ctx, head = ("zl", "y", "x"), ("zh", "core")
    return jax.shard_map(
        per_device,
        mesh=split,
        in_specs=(P(ctx, head), P(None, ctx, head), P(ctx), P()),
        out_specs=P(ctx + head, None),
        check_vma=False,
    )
```

```python
import functools
import math

import jax
import jax.numpy as jnp
from jax import lax
from jax.experimental import pallas as pl
from jax.experimental.pallas import tpu as pltpu
from jax.sharding import Mesh, PartitionSpec as P


HEAD_DIM = 128
SLOTS = 512
WIDTH = 512
SCALING = 1.0 / math.sqrt(HEAD_DIM)
LOG2E = math.log2(math.e)
MASKED = -1e30
CODE = 2 * SLOTS


def attend_kernel(along, coords, offset_ref, *refs):
    q_refs, kv_refs, out_ref = refs[:4], refs[4:12], refs[12]
    kbuf, vbuf, score0, score1, peak0, peak1, acc, logs, count = refs[13:]
    if coords is None:
        zl, y, x = lax.axis_index("zl"), lax.axis_index("y"), lax.axis_index("x")
    else:
        zl, y, x = coords
    offset = offset_ref[0]
    mine = y if along == "y" else x

    def ctx_of(z, step):
        return z * 16 + (step * 4 + x if along == "y" else y * 4 + step)

    other = x if along == "y" else y
    groups, places = [], []
    for k in range(4):
        g = (other + 4 - k) & 3
        places.append(pl.multiple_of(g * 32, 32))
        groups.append(zl * 16 + (y * 4 + g if along == "y" else g * 4 + x))
    first_token = offset + (zl * 16 + (y * 4 if along == "y" else x)) * 32
    last_token = first_token + 31 + (3 * 32 if along == "y" else 12 * 32)

    shard, fill, room = [], [], []
    for k in range(8):
        j = ctx_of(zl if k < 4 else 1 - zl, (mine + 4 - (k & 3)) & 3)
        code = kv_refs[k][CODE : CODE + 16, :].astype(jnp.float32)
        n = jnp.max(code[0:8]).astype(jnp.int32) * 16 + jnp.max(code[8:16]).astype(jnp.int32)
        n = jnp.where(j * SLOTS > last_token, 0, n)
        shard.append(j)
        fill.append(n)
        room.append(((n + 15) >> 4) << 4)
    start = []
    for k in range(8):
        before = jnp.int32(0)
        for o in range(8):
            if o != k:
                before = before + jnp.where(shard[o] < shard[k], room[o], 0)
        start.append(before)
    total = functools.reduce(lambda a, b: a + b, room)

    row = lax.broadcasted_iota(jnp.int32, (SLOTS, HEAD_DIM), 0)
    ones = jnp.ones((SLOTS, HEAD_DIM), jnp.bfloat16)
    zeros = jnp.zeros((SLOTS, HEAD_DIM), jnp.bfloat16)

    def pack(k):
        live = row < fill[k]
        at = pl.ds(pl.multiple_of(start[k], 16), SLOTS)
        keys = kv_refs[k][0:SLOTS, :]
        kbuf[at, :] = jnp.where(live, keys, jnp.broadcast_to(kv_refs[k][0:1, :], keys.shape))
        vbuf[at, 0:HEAD_DIM] = jnp.where(live, kv_refs[k][SLOTS : 2 * SLOTS, :], zeros)
        vbuf[at, HEAD_DIM:] = jnp.where(live, ones, zeros)

    for half in range(2):
        for step in range(4):
            for k in range(8):
                is_half = (zl if k < 4 else 1 - zl) == half
                is_step = ((mine + 4 - (k & 3)) & 3) == step
                pl.when(is_half & is_step & (fill[k] > 0))(functools.partial(pack, k))
    rest = pl.ds(pl.multiple_of(total, 16), WIDTH)
    kbuf[rest, :] = zeros
    vbuf[rest, 0:HEAD_DIM] = zeros
    vbuf[rest, HEAD_DIM:] = zeros

    token = lax.broadcasted_iota(jnp.int32, (32, HEAD_DIM), 0)
    for i in range(4):
        position = offset + groups[i] * 32 + token
        seen = jnp.zeros((32, HEAD_DIM), jnp.int32)
        for k in range(8):
            seen = seen + jnp.clip(position + 1 - shard[k] * SLOTS, 0, room[k])
        count[32 * i : 32 * i + 32, :] = seen
        count[128 + 32 * i : 160 + 32 * i, :] = seen
    least = jnp.int32(0)
    for k in range(8):
        least = least + jnp.clip(first_token + 1 - shard[k] * SLOTS, 0, room[k])
    clear = least // WIDTH
    blocks = (total + WIDTH - 1) // WIDTH
    logs[...] = jnp.zeros_like(logs)
    lane = lax.broadcasted_iota(jnp.int32, (256, HEAD_DIM), 1)
    lane_half = lax.broadcasted_iota(jnp.int32, (128, HEAD_DIM), 1)

    def queries_of(p):
        parts = []
        for h in range(2):
            cols = pl.ds(pl.multiple_of((2 * p + h) * HEAD_DIM, HEAD_DIM), HEAD_DIM)
            parts += [ref[:, cols] for ref in q_refs]
        return jnp.concatenate(parts, axis=0)

    def score(query, b, scores, peak, masked):
        at = pl.ds(pl.multiple_of(b * WIDTH, WIDTH), WIDTH)
        value = lax.dot_general(query, kbuf[at, :], (((1,), (1,)), ((), ())), preferred_element_type=jnp.float32)
        tiles = [value[:, 128 * t : 128 * t + 128] for t in range(WIDTH // 128)]
        if masked:
            limit = count[...] - b * WIDTH
            tiles = [jnp.where(lane + 128 * t < limit, tile, MASKED) for t, tile in enumerate(tiles)]
        top = peak[...]
        for t, tile in enumerate(tiles):
            scores[b, :, 128 * t : 128 * t + 128] = tile
            top = jnp.maximum(top, tile)
        peak[...] = top

    def weigh(b, scores, peak):
        at = pl.ds(pl.multiple_of(b * WIDTH, WIDTH), WIDTH)
        top = peak[...]
        weights = [
            jnp.exp2((scores[b, :, 128 * t : 128 * t + 128] - top) * (SCALING * LOG2E)).astype(jnp.bfloat16)
            for t in range(WIDTH // 128)
        ]
        acc[...] += jnp.dot(jnp.concatenate(weights, axis=1), vbuf[at, :], preferred_element_type=jnp.float32)

    def settle(peak):
        peak[...] = jnp.broadcast_to(jnp.max(peak[...], axis=1, keepdims=True), (256, HEAD_DIM))

    def finish(p, peak):
        mass = acc[:, HEAD_DIM:]
        partial = (acc[:, 0:HEAD_DIM] / mass).astype(jnp.bfloat16)
        log_total = peak[...] * SCALING + jnp.log(mass)
        for h in range(2):
            cols = pl.ds(pl.multiple_of((2 * p + h) * HEAD_DIM, HEAD_DIM), HEAD_DIM)
            for i in range(4):
                lo = 128 * h + 32 * i
                out_ref[pl.ds(places[i], 32), cols] = partial[lo : lo + 32]
            logs[...] = jnp.where(lane_half == 2 * p + h, log_total[128 * h : 128 * h + 128], logs[...])

    def stage(p, new, old):
        if new is not None:
            new[1][...] = jnp.full((256, HEAD_DIM), MASKED, jnp.float32)
            query = queries_of(p)
        if old is not None:
            acc[...] = jnp.zeros_like(acc)

        def body(b, masked):
            if old is not None:
                weigh(b, *old)
            if new is not None:
                score(query, b, *new, masked)

        def plain(b, c):
            body(b, False)
            return c

        def edged(b, c):
            body(b, True)
            return c

        if new is None:
            lax.fori_loop(0, blocks, plain, 0)
        else:
            lax.fori_loop(0, clear, plain, 0)
            lax.fori_loop(clear, blocks, edged, 0)
            settle(new[1])
        if old is not None:
            finish(p - 1, old[1])

    first, second = (score0, peak0), (score1, peak1)
    stage(0, first, None)

    def two(i, c):
        stage(2 * i + 1, second, first)
        stage(2 * i + 2, first, second)
        return c

    lax.fori_loop(0, 3, two, 0)
    stage(7, second, first)
    stage(8, None, second)

    value = logs[...]
    high = value.astype(jnp.bfloat16).astype(jnp.float32)
    left = value - high
    middle = left.astype(jnp.bfloat16).astype(jnp.float32)
    low = (left - middle).astype(jnp.bfloat16).astype(jnp.float32)
    packed = (high + pltpu.roll(middle, 32, 1) + pltpu.roll(low, 64, 1)).astype(jnp.bfloat16)
    for i in range(4):
        out_ref[pl.ds(places[i], 32), 2048:2176] = packed[32 * i : 32 * i + 32]


def attend(along, offset, q_pieces, kv_pieces, coords=None):
    room = 8 * SLOTS
    return pl.pallas_call(
        functools.partial(attend_kernel, along, coords),
        out_shape=jax.ShapeDtypeStruct((128, 2176), jnp.bfloat16),
        in_specs=[pl.BlockSpec(memory_space=pltpu.SMEM)] + [pl.BlockSpec(memory_space=pltpu.VMEM)] * 12,
        out_specs=pl.BlockSpec(memory_space=pltpu.VMEM),
        scratch_shapes=[
            pltpu.VMEM((room + WIDTH, HEAD_DIM), jnp.bfloat16),
            pltpu.VMEM((room + WIDTH, 2 * HEAD_DIM), jnp.bfloat16),
            pltpu.VMEM((room // WIDTH, 256, WIDTH), jnp.float32),
            pltpu.VMEM((room // WIDTH, 256, WIDTH), jnp.float32),
            pltpu.VMEM((256, HEAD_DIM), jnp.float32),
            pltpu.VMEM((256, HEAD_DIM), jnp.float32),
            pltpu.VMEM((256, 2 * HEAD_DIM), jnp.float32),
            pltpu.VMEM((128, HEAD_DIM), jnp.float32),
            pltpu.VMEM((256, HEAD_DIM), jnp.int32),
        ],
    )(offset, *q_pieces, *kv_pieces)


def merge_kernel(first_ref, second_ref, out_ref):
    for side, in_ref in enumerate((first_ref, second_ref)):
        totals = []
        for s in range(4):
            code = in_ref[s, 0, :, 2048:2176].astype(jnp.float32)
            totals.append(code + pltpu.roll(code, 96, 1) + pltpu.roll(code, 64, 1))
        peak = functools.reduce(jnp.maximum, totals)
        shares = [jnp.exp(t - peak) for t in totals]
        mass = shares[0] + shares[1] + shares[2] + shares[3]
        shares = [s / mass for s in shares]
        for h in range(16):
            cols = slice(h * HEAD_DIM, (h + 1) * HEAD_DIM)
            total = jnp.zeros((8, HEAD_DIM), jnp.float32)
            for s in range(4):
                share = jnp.broadcast_to(shares[s][:, h : h + 1], (8, HEAD_DIM))
                total = total + share * in_ref[s, 0, :, cols].astype(jnp.float32)
            at = side * 2048 + h * HEAD_DIM
            out_ref[:, at : at + HEAD_DIM] = total.astype(jnp.bfloat16)


def merge(first, second):
    block = pl.BlockSpec((4, 1, 8, 2176), lambda g: (0, g, 0, 0))
    return pl.pallas_call(
        merge_kernel,
        grid=(4,),
        out_shape=jax.ShapeDtypeStruct((8, 16384), jnp.bfloat16),
        in_specs=[block, block],
        out_specs=pl.BlockSpec((8, 4096), lambda g: (0, g)),
        name="merge",
    )(first, second)


def shift(value, axis, by):
    size = lax.axis_size(axis)
    return lax.ppermute(value, axis, [(i, (i + by) % size) for i in range(size)])


def per_device(queries, kv_cache, fill_len, prompt_offset):
    fill = fill_len[0]
    code = jnp.concatenate(
        [jnp.full((8, HEAD_DIM), fill // 16, jnp.bfloat16), jnp.full((8, HEAD_DIM), fill % 16, jnp.bfloat16)], axis=0
    )
    parts = []
    for part, (along, other) in enumerate((("y", "x"), ("x", "y"))):
        cols = slice(part * HEAD_DIM, (part + 1) * HEAD_DIM)
        cache = jnp.concatenate([kv_cache[0, :, cols], kv_cache[1, :, cols], code], axis=0)
        query = queries[:, part * 2048 : (part + 1) * 2048]

        across = shift(cache, "zl", 1)
        q_pieces = [query] + [shift(query, other, k) for k in (1, 2, 3)]
        kv_pieces = [cache] + [shift(cache, along, k) for k in (1, 2, 3)]
        kv_pieces += [across] + [shift(across, along, k) for k in (1, 2, 3)]
        parts.append((along, other, q_pieces, kv_pieces))
    received = []
    for along, other, q_pieces, kv_pieces in parts:
        partial = attend(along, prompt_offset, q_pieces, kv_pieces)
        swapped = lax.all_to_all(
            partial.reshape(16, 8, 2176), (other, "zh", "core"), split_axis=0, concat_axis=0, tiled=True
        )
        received.append(swapped.reshape(4, 4, 8, 2176))
    return merge(*received)


def solution(mesh):
    split = Mesh(mesh.devices.reshape(2, 4, 4, 2, 2), ("zl", "y", "x", "zh", "core"))
    ctx, head = ("zl", "y", "x"), ("zh", "core")
    return jax.shard_map(
        per_device,
        mesh=split,
        in_specs=(P(ctx, head), P(None, ctx, head), P(ctx), P()),
        out_specs=P(ctx + head, None),
        check_vma=False,
    )
```
